32 devices in a mesh: ctx: 16 (over z, x, core), head: 2 (over y).
Axes of the slice: x: 2, y: 2, z: 4, core: 2. Of those that a mesh axis runs over, the one named last changes fastest.
Arguments:
- queries: bfloat16 [16384, 4096], P(('ctx', 'head')), may hold values from -64 to 64
- keys: bfloat16 [16384, 1024], P(('ctx', 'head')), may hold values from -16 to 16
- values: bfloat16 [16384, 1024], P(('ctx', 'head')), may hold values from -6 to 6
- column_blocks: int32 [32, 12], replicated, may hold values from 0 to 255, as said below
- doc_lengths: int32 [16], replicated, may hold values from 1 to 15872, as said below
Outputs:
- attention: bfloat16 [16384, 4096], P(('ctx', 'head'))
The draws below stay inside these ranges and needn't reach their ends.
Inputs may be any that keep to these rules, and one draw needn't show every extreme that they name: `column_blocks`: for each of the 8 key-value heads, the 48 blocks listed by its query heads are distinct, at most 3 of them lie in one shard of 1024 tokens, and some shard holds exactly 3 of them. `doc_lengths`: the first rollout holds 15872 tokens; the other rollouts share the remaining tokens, each at least one.
All inputs are finite; a program needn't handle non-finite values.
Results may differ from the reference program's by a relative error of at most 0.0042.
Values may be sent and summed in bfloat16 or wider, within the bound.
No kernel may reach another device: no remote copies, remote signals or barrier semaphores. Data moves between devices by JAX's collectives and lax.ppermute only.
A program may use at most 64 MiB of HBM per device.

```python
import math
import jax
import jax.numpy as jnp
from jax import lax

HQ = 32
KEY_VALUE_HEADS = 8
HEAD_SIZE = 128
S_DEV = 1024
BAND = 1024
BLK = 64
NV = 12
QBLK = 512
NDOC = 16
GQ = 4
TOKEN_TOTAL = 16384
CAP = 3
N_CTX = 16


def draw_queries(key, part):
    attention_output = jnp.clip(jax.random.normal(jax.random.fold_in(key, 1), (TOKEN_TOTAL, HQ * HEAD_SIZE), jnp.float32), -6.0, 6.0)
    return attention_output.astype(jnp.bfloat16)


def draw_keys(key, part):
    attention_output = jnp.clip(jax.random.normal(jax.random.fold_in(key, 2), (TOKEN_TOTAL, KEY_VALUE_HEADS * HEAD_SIZE), jnp.float32), -6.0, 6.0)
    return attention_output.astype(jnp.bfloat16)


def draw_column_blocks(key, part):
    per_shard = S_DEV // BLK
    entry_count = GQ * NV
    slot_total = N_CTX * CAP
    slot_ids = jnp.arange(slot_total, dtype=jnp.int32)
    lists = []
    for query_group in range(KEY_VALUE_HEADS):
        group_key = jax.random.fold_in(key, 100 + query_group)
        order = jax.random.permutation(jax.random.fold_in(group_key, 1), slot_ids)
        inverse = jnp.zeros((slot_total,), jnp.int32).at[order].set(slot_ids)
        first_owner = order[0] // CAP
        score_ints = jnp.where(slot_ids // CAP == first_owner, slot_ids % CAP - CAP, inverse)
        score_ints = jnp.where(slot_ids == 0, -CAP - 1, score_ints)
        chosen = jnp.argsort(score_ints, stable=True)[:entry_count]
        owner_ids = chosen // CAP
        rank_ids = chosen % CAP
        shift_ids = jax.random.randint(jax.random.fold_in(group_key, 2), (N_CTX,), 0, per_shard)
        local_ids = (shift_ids[owner_ids] + rank_ids) % per_shard
        block_ids = owner_ids * per_shard + local_ids
        mixing = jax.random.permutation(jax.random.fold_in(group_key, 3), jnp.arange(entry_count, dtype=jnp.int32))
        lists.append(block_ids[mixing].reshape(GQ, NV))
    return jnp.concatenate(lists, axis=0).astype(jnp.int32)


def draw_doc_lengths(key, part):
    remaining = S_DEV // 2
    spare = remaining - (NDOC - 1)
    picks = jax.random.randint(jax.random.fold_in(key, 11), (max(spare, 1),), 0, NDOC - 1)
    tallies = jnp.sum((picks[:, None] == jnp.arange(NDOC - 1, dtype=jnp.int32)[None, :]).astype(jnp.int32), axis=0)
    tallies = tallies * (1 if spare > 0 else 0)
    first_len = jnp.full((1,), TOKEN_TOTAL - remaining, jnp.int32)
    return jnp.concatenate([first_len, 1 + tallies]).astype(jnp.int32)


def levels(key, extent, split, low, top_value):
    def one(position, blocks):
        steps = jax.random.uniform(jax.random.fold_in(jax.random.fold_in(key, 6), position), (blocks,), jnp.float32, low / len(split), top_value / len(split))
        return jnp.repeat(jnp.exp(steps), extent[position] // blocks).reshape((-1,) + (1,) * (len(extent) - position - 1))

    loudness = one(*split[0])
    for cut in split[1:]:
        loudness = loudness * one(*cut)
    return loudness


def noise(own_key, extent, width, most, shards=(), kind=jnp.bfloat16):
    array = width * jax.random.normal(own_key, extent, jnp.float32)
    if shards:
        array = array * levels(own_key, extent, shards, -0.22, 0.18)
    return jnp.clip(array, -most, most).astype(kind)


def setup_inputs(seed: int = 0) -> dict:
    streams_of = jax.random.split(jax.random.key(seed), 6)
    queries = draw_queries(jax.random.fold_in(streams_of[5], 71), 0)
    keys = draw_keys(jax.random.fold_in(streams_of[5], 71), 0)
    values = noise(streams_of[2], (TOKEN_TOTAL, KEY_VALUE_HEADS * HEAD_SIZE), 1.0, 6.0, ((0, 32),))
    column_blocks = draw_column_blocks(jax.random.fold_in(streams_of[5], 71), 0)
    doc_lengths = draw_doc_lengths(jax.random.fold_in(streams_of[5], 71), 0)
    return dict(queries=queries, keys=keys, values=values, column_blocks=column_blocks, doc_lengths=doc_lengths)


def segment_of(positions, doc_ends):
    return lax.optimization_barrier(jnp.sum((doc_ends[None, :] <= positions[:, None]).astype(jnp.int32), axis=1))

def rows_product(left, right):
    return lax.dot_general(left, right, (((1,), (1,)), ((), ())), preferred_element_type=jnp.float32)

def block_attention(query_rows, query_pos, band_keys, band_vals, band_pos, column_keys, column_vals, column_pos, doc_ends):
    score_scale = 1.0 / math.sqrt(query_rows.shape[1])
    query_seg = segment_of(query_pos, doc_ends)
    band_gap = query_pos[:, None] - band_pos[None, :]
    band_mask = (band_gap >= 0) & (band_gap < BAND) & (band_pos[None, :] >= 0) & (query_seg[:, None] == segment_of(band_pos, doc_ends)[None, :])
    column_gap = query_pos[:, None] - column_pos[None, :]
    column_mask = (column_gap >= BAND) & (query_seg[:, None] == segment_of(column_pos, doc_ends)[None, :])
    band_scores = jnp.where(band_mask, rows_product(query_rows, band_keys) * score_scale, -jnp.inf)
    column_scores = jnp.where(column_mask, rows_product(query_rows, column_keys) * score_scale, -jnp.inf)
    row_peak = jnp.maximum(lax.optimization_barrier(jnp.max(band_scores, axis=1)), lax.optimization_barrier(jnp.max(column_scores, axis=1)))
    band_prob = jnp.exp(band_scores - row_peak[:, None])
    column_prob = jnp.exp(column_scores - row_peak[:, None])
    denominator = lax.optimization_barrier(jnp.sum(band_prob, axis=1)) + lax.optimization_barrier(jnp.sum(column_prob, axis=1))
    numerator = jnp.dot(band_prob.astype(jnp.bfloat16), band_vals, preferred_element_type=jnp.float32)
    numerator = numerator + jnp.dot(column_prob.astype(jnp.bfloat16), column_vals, preferred_element_type=jnp.float32)
    return (numerator / denominator[:, None]).astype(jnp.bfloat16)

def group_attention(group_queries, ext_keys, ext_vals, vert_keys, vert_vals, vert_pos, row_start, doc_ends):
    row_count = group_queries.shape[0]
    block_count = row_count // QBLK
    band_span = jnp.arange(BAND + QBLK, dtype=jnp.int32)
    query_span = jnp.arange(QBLK, dtype=jnp.int32)

    def one_block(item_index):
        head_slot = item_index // block_count
        block_index = item_index % block_count
        first_row = block_index * QBLK
        query_rows = lax.dynamic_slice(group_queries, (first_row, head_slot * HEAD_SIZE), (QBLK, HEAD_SIZE))
        band_keys = lax.dynamic_slice_in_dim(ext_keys, first_row, BAND + QBLK, 0)
        band_vals = lax.dynamic_slice_in_dim(ext_vals, first_row, BAND + QBLK, 0)
        query_pos = row_start + first_row + query_span
        band_pos = row_start + first_row - BAND + band_span
        return block_attention(query_rows, query_pos, band_keys, band_vals, band_pos, vert_keys[head_slot], vert_vals[head_slot], vert_pos[head_slot], doc_ends)
    blocks = lax.map(one_block, jnp.arange(GQ * block_count, dtype=jnp.int32))
    return blocks.reshape(GQ, row_count, HEAD_SIZE).transpose(1, 0, 2).reshape(row_count, GQ * HEAD_SIZE)

def reference(queries, keys, values, column_blocks, doc_lengths):
    doc_ends = jnp.cumsum(doc_lengths).astype(jnp.int32)
    zero_rim = jnp.zeros((BAND, keys.shape[1]), keys.dtype)
    ext_keys = jnp.concatenate([zero_rim, keys], axis=0)
    ext_vals = jnp.concatenate([zero_rim, values], axis=0)
    offsets = jnp.arange(BLK, dtype=jnp.int32)
    outputs = []
    for query_group in range(KEY_VALUE_HEADS):
        block_ids = column_blocks[query_group * GQ:(query_group + 1) * GQ]
        vert_pos = (block_ids[:, :, None] * BLK + offsets[None, None, :]).reshape(GQ, NV * BLK)
        key_cols = keys[:, query_group * HEAD_SIZE:(query_group + 1) * HEAD_SIZE]
        value_cols = values[:, query_group * HEAD_SIZE:(query_group + 1) * HEAD_SIZE]
        vert_keys = jnp.take(key_cols, vert_pos.reshape(-1), axis=0).reshape(GQ, NV * BLK, HEAD_SIZE)
        vert_vals = jnp.take(value_cols, vert_pos.reshape(-1), axis=0).reshape(GQ, NV * BLK, HEAD_SIZE)
        outputs.append(group_attention(queries[:, query_group * GQ * HEAD_SIZE:(query_group + 1) * GQ * HEAD_SIZE], ext_keys[:, query_group * HEAD_SIZE:(query_group + 1) * HEAD_SIZE], ext_vals[:, query_group * HEAD_SIZE:(query_group + 1) * HEAD_SIZE], vert_keys, vert_vals, vert_pos, 0, doc_ends))
    return jnp.concatenate(outputs, axis=1)
```

```python
import functools
import math

import jax
import jax.numpy as jnp
from jax import lax
from jax.experimental import pallas as pl
from jax.experimental.pallas import tpu as pltpu
from jax.sharding import PartitionSpec as P

HEAD_SIZE = 128
BAND = 1024
BLK = 64
NV = 12
GQ = 4
MINUS = float("-inf")
SCALE = math.log2(math.e) / math.sqrt(HEAD_SIZE)


def rows_product(left, right):
    return lax.dot_general(
        left, right, (((1,), (1,)), ((), ())), preferred_element_type=jnp.float32
    )


def pick_kernel(rows_ref, head_ref, k_ref, v_ref, out_ref):
    n_head, _, height, width = out_ref.shape
    capacity = height // BLK
    groups = width // HEAD_SIZE
    for g in range(n_head * groups):
        ahead = lax.rem(g // groups - head_ref[0] + n_head, n_head)
        cols = slice((g % groups) * HEAD_SIZE, (g % groups + 1) * HEAD_SIZE)
        own_cols = slice(g * HEAD_SIZE, (g + 1) * HEAD_SIZE)
        for s in range(capacity):
            row = rows_ref[g * capacity + s]
            start = pl.multiple_of(jnp.maximum(row, 0), BLK)
            for kv, ref in enumerate((k_ref, v_ref)):
                block = ref[pl.ds(start, BLK), own_cols]
                out_ref[ahead, kv, s * BLK : (s + 1) * BLK, cols] = jnp.where(
                    row >= 0, block, jnp.zeros_like(block)
                )


def segments(positions, ends_ref):
    seg = jnp.zeros_like(positions)
    for d in range(ends_ref.shape[0]):
        seg = seg + jnp.where(ends_ref[d] <= positions, 1, 0)
    return seg


def band_kernel(n_rims, place_ref, ends_ref, q_ref, *refs):
    parts = n_rims + 1
    k_refs, v_refs = refs[:parts], refs[parts : 2 * parts]
    acc_ref, ml_ref, kext, vext = refs[2 * parts :]
    rows = q_ref.shape[0]
    tile = min(256, rows)

    @pl.when(pl.program_id(0) == 0)
    def _():
        vext[:, HEAD_SIZE:] = jnp.ones((vext.shape[0], HEAD_SIZE), vext.dtype)

    for n in range(parts):
        kext[n * rows : (n + 1) * rows, :] = k_refs[n][...]
        vext[n * rows : (n + 1) * rows, :HEAD_SIZE] = v_refs[n][...]

    span = BAND + tile
    lanes = lax.broadcasted_iota(jnp.int32, (tile, HEAD_SIZE), 1)

    def unit(h, r0, masked):
        cols = pl.ds(pl.multiple_of(h * HEAD_SIZE, HEAD_SIZE), HEAD_SIZE)
        scores = rows_product(q_ref[r0 : r0 + tile, cols], kext[r0 : r0 + span, :])
        scores = masked(scores, r0)
        peak = jnp.max(scores, axis=1, keepdims=True)
        prob = jnp.exp2((scores - peak) * SCALE).astype(jnp.bfloat16)
        total = jnp.dot(prob, vext[r0 : r0 + span, :], preferred_element_type=jnp.float32)
        acc_ref[r0 : r0 + tile, cols] = total[:, :HEAD_SIZE]
        old = ml_ref[r0 : r0 + tile, :]
        new = jnp.where(
            lanes // 16 == 2 * h, peak, jnp.where(lanes // 16 == 2 * h + 1, total[:, HEAD_SIZE:], old)
        )
        ml_ref[r0 : r0 + tile, :] = new

    def plain_mask(scores, r0):
        del r0
        row = lax.broadcasted_iota(jnp.int32, (tile, tile), 0)
        col = lax.broadcasted_iota(jnp.int32, (tile, tile), 1)
        first = jnp.where(col > row, scores[:, :tile], MINUS)
        last = jnp.where(col <= row, scores[:, BAND:], MINUS)
        return jnp.concatenate([first, scores[:, tile:BAND], last], axis=1)

    def full_mask(scores, r0):
        start = place_ref[0] + r0
        row = lax.broadcasted_iota(jnp.int32, (tile, 1), 0)
        col = lax.broadcasted_iota(jnp.int32, (1, span), 1)
        row_seg = segments(row + start, ends_ref)
        col_seg = segments(col + start - BAND, ends_ref)
        keep = (col > row) & (col <= row + BAND) & (col + start >= BAND) & (row_seg == col_seg)
        return jnp.where(keep, scores, MINUS)

    def all_units(masked):
        def step(h, carry):
            for r0 in range(0, rows, tile):
                unit(h, r0, masked)
            return carry

        lax.fori_loop(0, GQ, step, 0)

    @pl.when(place_ref[1] == 0)
    def _():
        all_units(plain_mask)

    @pl.when(place_ref[1] != 0)
    def _():
        all_units(full_mask)


def column_kernel(
    place_ref, owner_ref, rank_ref, live_ref, q_ref, limit_ref, blocks_ref, acc_ref, ml_ref, out_ref, kbuf, vbuf
):
    rows = q_ref.shape[0]
    tile = min(256, rows)
    height = blocks_ref.shape[2] // 2
    g = pl.program_id(0)
    wide = NV * BLK

    @pl.when(g == 0)
    def _():
        vbuf[:, HEAD_SIZE:] = jnp.ones((wide, HEAD_SIZE), vbuf.dtype)

    for h in range(GQ):
        cols = slice(h * HEAD_SIZE, (h + 1) * HEAD_SIZE)
        live = live_ref[g * GQ + h]

        @pl.when(live != 0)
        def _():
            for n in range(NV):
                entry = (g * GQ + h) * NV + n
                owner = owner_ref[entry]
                row = pl.multiple_of(rank_ref[entry] * BLK, BLK)
                kbuf[n * BLK : (n + 1) * BLK, :] = blocks_ref[owner, 0, pl.ds(row, BLK), :]
                vbuf[n * BLK : (n + 1) * BLK, :HEAD_SIZE] = blocks_ref[
                    owner, 0, pl.ds(row + height, BLK), :
                ]
            for r0 in range(0, rows, tile):
                row = lax.broadcasted_iota(jnp.int32, (tile, 1), 0) + r0
                reach = jnp.where(row < place_ref[1], row, -(2**30))
                scores = rows_product(q_ref[r0 : r0 + tile, cols], kbuf[...])
                scores = jnp.where(limit_ref[h] <= reach, scores, MINUS)
                state = ml_ref[r0 : r0 + tile, :]
                old_peak = state[:, 32 * h : 32 * h + 1]
                old_sum = state[:, 32 * h + 16 : 32 * h + 17]
                peak = jnp.maximum(old_peak, jnp.max(scores, axis=1, keepdims=True))
                prob = jnp.exp2((scores - peak) * SCALE).astype(jnp.bfloat16)
                keep = jnp.exp2((old_peak - peak) * SCALE)
                total = jnp.dot(prob, vbuf[...], preferred_element_type=jnp.float32)
                acc = acc_ref[r0 : r0 + tile, cols] * keep + total[:, :HEAD_SIZE]
                denom = old_sum * keep + total[:, HEAD_SIZE:]
                out_ref[r0 : r0 + tile, cols] = (acc / denom).astype(out_ref.dtype)

        @pl.when(live == 0)
        def _():
            for r0 in range(0, rows, tile):
                old_sum = ml_ref[r0 : r0 + tile, 32 * h + 16 : 32 * h + 17]
                out_ref[r0 : r0 + tile, cols] = (acc_ref[r0 : r0 + tile, cols] / old_sum).astype(
                    out_ref.dtype
                )


def per_device(queries, keys, values, column_blocks, doc_lengths):
    axes = ("ctx", "head")
    n_ctx, n_head = lax.axis_size("ctx"), lax.axis_size("head")
    n_dev = n_ctx * n_head
    rows = queries.shape[0]
    kv_heads = keys.shape[1] // HEAD_SIZE
    groups = kv_heads // n_head
    entries = GQ * NV
    capacity = max(2, (entries + n_ctx - 1) // n_ctx)
    height = capacity * BLK
    ctx_index, head_index = lax.axis_index("ctx"), lax.axis_index("head")
    device = ctx_index * n_head + head_index
    start = device * rows
    per_shard = rows * n_head // BLK

    listed = column_blocks.reshape(kv_heads, entries)
    owners = listed // per_shard
    order = jnp.arange(entries, dtype=jnp.int32)
    earlier = (owners[:, :, None] == owners[:, None, :]) & (order[:, None] > order[None, :])
    ranks = jnp.sum(earlier.astype(jnp.int32), axis=2)
    mine = (listed * BLK >= start) & (listed * BLK < start + rows)
    slots = jnp.arange(capacity, dtype=jnp.int32)
    chosen = mine[:, None, :] & (ranks[:, None, :] == slots[None, :, None])
    pick_rows = jnp.max(jnp.where(chosen, (listed * BLK - start)[:, None, :], -1), axis=2).reshape(-1)

    picked = pl.pallas_call(
        pick_kernel,
        out_shape=jax.ShapeDtypeStruct((n_head, 2, height, groups * HEAD_SIZE), jnp.bfloat16),
        in_specs=[pl.BlockSpec(memory_space=pltpu.SMEM)] * 2
        + [pl.BlockSpec(memory_space=pltpu.VMEM)] * 2,
        out_specs=pl.BlockSpec(memory_space=pltpu.VMEM),
        name="pick",
    )(pick_rows, head_index.reshape(1), keys, values)
    item = picked[0]
    for ahead in range(1, n_head):
        item = item + lax.ppermute(
            picked[ahead], "head", [(i, (i + ahead) % n_head) for i in range(n_head)]
        )

    n_rims = BAND // rows
    rim_keys, rim_values = [], []
    for back in range(n_rims, 0, -1):
        pairs = [(i, i + back) for i in range(n_dev - back)]
        rim_keys.append(lax.ppermute(keys, axes, pairs))
        rim_values.append(lax.ppermute(values, axes, pairs))
    gathered = lax.all_gather(item, axes, axis=0, tiled=False)
    gathered = gathered.reshape(n_ctx, n_head, 2 * height, groups * HEAD_SIZE)

    doc_ends = jnp.cumsum(doc_lengths).astype(jnp.int32)
    edge = (start < BAND) | (start + rows > doc_ends[0])
    band_place = jnp.stack([start, edge.astype(jnp.int32)]).astype(jnp.int32)
    ext_spec = [pl.BlockSpec((rows, HEAD_SIZE), lambda g, *_: (0, g))] * (n_rims + 1)
    wide_q = GQ * HEAD_SIZE
    state, ml = pl.pallas_call(
        functools.partial(band_kernel, n_rims),
        out_shape=(
            jax.ShapeDtypeStruct(queries.shape, jnp.float32),
            jax.ShapeDtypeStruct((rows, kv_heads * HEAD_SIZE), jnp.float32),
        ),
        grid_spec=pltpu.PrefetchScalarGridSpec(
            num_scalar_prefetch=2,
            grid=(kv_heads,),
            in_specs=[pl.BlockSpec((rows, wide_q), lambda g, *_: (0, g))] + ext_spec + ext_spec,
            out_specs=(
                pl.BlockSpec((rows, wide_q), lambda g, *_: (0, g)),
                pl.BlockSpec((rows, HEAD_SIZE), lambda g, *_: (0, g)),
            ),
            scratch_shapes=[
                pltpu.VMEM((BAND + rows, HEAD_SIZE), jnp.bfloat16),
                pltpu.VMEM((BAND + rows, 2 * HEAD_SIZE), jnp.bfloat16),
            ],
        ),
        cost_estimate=pl.CostEstimate(
            flops=rows * 4096 * 1280 * 4, bytes_accessed=rows * 4096 * 8, transcendentals=0
        ),
        name="band",
    )(band_place, doc_ends, queries, *rim_keys, keys, *rim_values, values)

    offsets = jnp.arange(BLK, dtype=jnp.int32)
    limits = (column_blocks[:, :, None] * BLK + offsets + (BAND - start)).reshape(-1, 1, NV * BLK)
    live = jnp.any(column_blocks * BLK + BAND < start + rows, axis=1) & (start < doc_ends[0])
    column_place = jnp.stack([start, doc_ends[0] - start]).astype(jnp.int32)
    return pl.pallas_call(
        column_kernel,
        out_shape=jax.ShapeDtypeStruct(queries.shape, jnp.bfloat16),
        grid_spec=pltpu.PrefetchScalarGridSpec(
            num_scalar_prefetch=4,
            grid=(kv_heads,),
            in_specs=[
                pl.BlockSpec((rows, wide_q), lambda g, *_: (0, g)),
                pl.BlockSpec((GQ, 1, NV * BLK), lambda g, *_: (g, 0, 0)),
                pl.BlockSpec(
                    (n_ctx, 1, 2 * height, HEAD_SIZE),
                    lambda g, *_: (0, g // groups, 0, g % groups),
                ),
                pl.BlockSpec((rows, wide_q), lambda g, *_: (0, g)),
                pl.BlockSpec((rows, HEAD_SIZE), lambda g, *_: (0, g)),
            ],
            out_specs=pl.BlockSpec((rows, wide_q), lambda g, *_: (0, g)),
            scratch_shapes=[
                pltpu.VMEM((NV * BLK, HEAD_SIZE), jnp.bfloat16),
                pltpu.VMEM((NV * BLK, 2 * HEAD_SIZE), jnp.bfloat16),
            ],
        ),
        name="columns",
    )(
        column_place,
        owners.reshape(-1),
        ranks.reshape(-1),
        live.astype(jnp.int32),
        queries,
        limits,
        gathered,
        state,
        ml,
    )


def solution(mesh):
    placed = (
        P(("ctx", "head"), None),
        P(("ctx", "head"), None),
        P(("ctx", "head"), None),
        P(),
        P(),
    )
    return jax.shard_map(
        per_device, mesh=mesh, in_specs=placed, out_specs=P(("ctx", "head"), None), check_vma=False
    )
```
